256 devices in a mesh: tm: 8 (over x_hi, y), chan: 32 (over z, x_lo, core).
Axes of the slice: x: 4 (x_hi: 2, x_lo: 2; x = x_hi * 2 + x_lo), y: 4, z: 8, core: 2. Of those that a mesh axis runs over, the one named last changes fastest.
Arguments:
- vis: bfloat16 [512, 1024, 512], P('tm', 'chan'), may hold values from -6 to 6
- beam: bfloat16 [16, 1024, 2, 64, 256], P('tm', 'chan'), may hold values from -0.25 to 0.25
- fg_cov: float32 [1024, 1024], replicated, may hold values from 0 to 30, as said below
- flags: int32 [1024], replicated, may hold values 0 or 1
- m_modes: int32 [16], replicated, may hold values from 0 to 255, as said below
Outputs:
- filled: float32 [16, 2, 64, 1024], P('tm', None, None, 'chan')
The draws below stay inside these ranges and needn't reach their ends.
Inputs may be any that keep to these rules, and one draw needn't show every extreme that they name: `m_modes`: m numbers of the window; entries may repeat. `fg_cov`: symmetric and positive definite.
All inputs are finite; a program needn't handle non-finite values.
Results may differ from the reference program's by a relative error of at most 0.0085.
Values sent between devices are 32-bit elements; how exact they have to be, the bound alone decides.
A program may use at most 64 MiB of HBM per device.

```python
import math
import jax
import jax.numpy as jnp
from jax import lax

NF = 1024
NB = 256
L = 64
M = 16
ITERS = 10
NT = 512


def draw_fg_cov(key, part):
    key_scale = jax.random.fold_in(key, 11)
    freq = jnp.arange(NF, dtype=jnp.float32) / NF
    smooth = (1.0 + freq) ** (-2.0)
    rough = jnp.exp(jax.random.uniform(key_scale, (NF,), jnp.float32, jnp.log(0.4), jnp.log(30.0)))
    weight_long, weight_short, weight_nugget = (0.6, 0.3, 0.5)
    scales = rough * smooth
    dist = jnp.abs(freq[:, None] - freq[None, :])
    rows = jnp.arange(NF)
    same = jnp.where(rows[:, None] == rows[None, :], 1.0, 0.0)
    spread = weight_long * jnp.exp(-dist / 0.4) + weight_short * jnp.exp(-dist / 0.03)
    kernel = 8.0 / NF * spread + weight_nugget * same
    root = jnp.sqrt(scales)
    return (root[:, None] * kernel * root[None, :]).astype(jnp.float32)


def draw_m_modes(key, part):
    half = NT // 2
    key_pick, key_slot = jax.random.split(jax.random.fold_in(key, 7))
    picks = jax.random.randint(key_pick, (M,), 0, half)
    order = jax.random.permutation(key_slot, M)
    picks = picks.at[order[0]].set(half - 1)
    picks = picks.at[order[1]].set(0)
    return picks.astype(jnp.int32)


def touch_ends(result, rng, least, high):
    longest = result.shape.index(max(result.shape))
    spots = []
    for shift in (0, 1):
        where = [jax.random.randint(jax.random.fold_in(rng, axis), (), 0, length) for axis, length in enumerate(result.shape)]
        where[longest] = (where[longest] + shift) % result.shape[longest]
        spots.append(tuple(where))
    return result.at[spots[0]].set(least).at[spots[1]].set(high)


def levels(stream_key, dims, pieces, least, largest):
    factor_of = 1.0
    for position, shards_of in pieces:
        steps = jax.random.uniform(jax.random.fold_in(jax.random.fold_in(stream_key, 6), position), (shards_of,), jnp.float32, least / len(pieces), largest / len(pieces))
        factor_of = factor_of * jnp.repeat(jnp.exp(steps), dims[position] // shards_of).reshape((-1,) + (1,) * (len(dims) - 1 - position))
    return factor_of


def normal_values(rng, dims, scale, most, cuts=(), kind=jnp.bfloat16):
    factor_of = levels(rng, dims, cuts, -0.22, 0.18) if cuts else 1.0
    entries = jax.random.normal(rng, dims, jnp.float32) * scale * factor_of
    return jnp.minimum(jnp.maximum(entries, -most), most).astype(kind)


def setup_inputs(seed: int = 0) -> dict:
    splits = jax.random.split(jax.random.key(seed), 6)
    vis = normal_values(splits[0], (NT, NF, 2 * NB), 1.0, 6.0, ((0, 8), (1, 32)))
    beam = normal_values(splits[1], (M, NF, 2, L, NB), (2 * NB) ** -0.5, 0.25, ((0, 8), (1, 32)))
    fg_cov = draw_fg_cov(jax.random.fold_in(splits[5], 71), 0)
    flags = touch_ends((jax.random.randint(splits[3], (NF,), 0, 4) < 1).astype(jnp.int32), jax.random.fold_in(splits[3], 1), 0, 1)
    m_modes = draw_m_modes(jax.random.fold_in(splits[5], 71), 0)
    return dict(vis=vis, beam=beam, fg_cov=fg_cov, flags=flags, m_modes=m_modes)


EPS = 1e-06

def conjugate_fill(rows, good, cov):

    def apply_cov(vec):
        return jnp.dot(vec, cov, precision=lax.Precision.HIGHEST, preferred_element_type=jnp.float32)

    def operator(vec):
        return vec + good * apply_cov(good * vec)
    start = good * rows
    norm_now = lax.optimization_barrier(jnp.sum(start * start, axis=1, keepdims=True))

    def advance(step, carry):
        sol, resid, direc, norm_now = carry
        image = operator(direc)
        alpha = norm_now / (lax.optimization_barrier(jnp.sum(direc * image, axis=1, keepdims=True)) + EPS)
        sol = sol + alpha * direc
        resid = resid - alpha * image
        norm_next = lax.optimization_barrier(jnp.sum(resid * resid, axis=1, keepdims=True))
        direc = resid + norm_next / (norm_now + EPS) * direc
        return (sol, resid, direc, norm_next)
    sol, resid, direc, norm_now = lax.fori_loop(0, ITERS, advance, (jnp.zeros_like(rows), start, start, norm_now))
    signal = apply_cov(good * sol)
    return good * rows + (1.0 - good) * signal

def reference(vis, beam, fg_cov, flags, m_modes):
    times = jnp.arange(NT, dtype=jnp.int32)
    index = m_modes[:, None] * times[None, :] % NT
    angle = 2.0 * math.pi / NT * index.astype(jnp.float32)
    tables = jnp.concatenate([jnp.cos(angle), jnp.sin(angle)], axis=0).astype(jnp.bfloat16)
    flat = vis.reshape(NT, NF * 2 * NB)
    prod = jnp.dot(tables, flat, preferred_element_type=jnp.float32).reshape(2, M, NF, 2 * NB)
    cos_part, sin_part = (prod[0], prod[1])
    scale = 1.0 / math.sqrt(NT)
    real_part = (cos_part[..., :NB] + sin_part[..., NB:]) * scale
    imag_part = (cos_part[..., NB:] - sin_part[..., :NB]) * scale
    mvis = jnp.concatenate([real_part, imag_part], axis=-1).astype(jnp.bfloat16)

    def project(pair):
        weights, data = pair
        prods = jnp.einsum('fpln,fqn->pqlf', weights.astype(jnp.float32), data.reshape(NF, 2, NB).astype(jnp.float32))
        return jnp.stack([prods[0, 0] - prods[1, 1], prods[1, 0] + prods[0, 1]], axis=0)
    coeffs = lax.map(project, (beam, mvis))
    good = (1 - flags).astype(jnp.float32)
    rows = coeffs.reshape(M * 2 * L, NF)
    return conjugate_fill(rows, good, fg_cov).reshape(M, 2, L, NF)
```

```python
import math

import jax
import jax.numpy as jnp
from jax import lax
from jax.sharding import PartitionSpec as P

ITERS = 10
EPS = 1e-06


def conjugate_fill(rows, good, cov):

    def apply_cov(vec):
        return jnp.dot(vec, cov, precision=lax.Precision.HIGHEST, preferred_element_type=jnp.float32)

    start = good * rows
    norm_now = jnp.sum(start * start, axis=1, keepdims=True)

    def advance(step, carry):
        sol, resid, direc, norm_now = carry
        image = direc + good * apply_cov(direc)
        alpha = norm_now / (jnp.sum(direc * image, axis=1, keepdims=True) + EPS)
        sol = sol + alpha * direc
        resid = resid - alpha * image
        norm_next = jnp.sum(resid * resid, axis=1, keepdims=True)
        direc = resid + norm_next / (norm_now + EPS) * direc
        return (sol, resid, direc, norm_next)

    sol, resid, direc, norm_now = lax.fori_loop(
        0, ITERS, advance, (jnp.zeros_like(rows), start, start, norm_now)
    )
    return start + (1.0 - good) * apply_cov(sol)


def per_device(vis, beam, fg_cov, flags, m_modes):
    t_dev = vis.shape[0]
    f_dev = vis.shape[1]
    width = vis.shape[2]
    half_width = width // 2
    n_time = t_dev * lax.axis_size("tm")
    m_dev = m_modes.shape[0] // lax.axis_size("tm")
    times = lax.axis_index("tm") * t_dev + jnp.arange(t_dev, dtype=jnp.int32)
    flat = vis.reshape(t_dev, f_dev * width)
    scale = 1.0 / math.sqrt(n_time)
    index = m_modes[:, None] * times[None, :] % n_time
    angle = 2.0 * math.pi / n_time * index.astype(jnp.float32)
    tables = jnp.concatenate([jnp.cos(angle), jnp.sin(angle)], axis=0).astype(jnp.bfloat16)
    prod = jnp.dot(tables, flat, preferred_element_type=jnp.float32).reshape(
        2, m_dev * lax.axis_size("tm"), f_dev, width
    )
    cos_part = prod[0]
    sin_part = prod[1]
    real_part = (cos_part[..., :half_width] + sin_part[..., half_width:]) * scale
    imag_part = (cos_part[..., half_width:] - sin_part[..., :half_width]) * scale
    mvis = lax.psum_scatter(
        jnp.concatenate([real_part, imag_part], axis=-1), "tm", scatter_dimension=0, tiled=True
    ).astype(jnp.bfloat16)
    prods = jnp.einsum(
        "mfpln,mfqn->mpqlf",
        beam,
        mvis.reshape(m_dev, f_dev, 2, half_width),
        preferred_element_type=jnp.float32,
    )
    coeffs = jnp.stack([prods[:, 0, 0] - prods[:, 1, 1], prods[:, 1, 0] + prods[:, 0, 1]], axis=1)
    degrees = coeffs.shape[2]
    good = (1 - flags).astype(jnp.float32)
    rows = coeffs.reshape(-1, f_dev)
    mine = lax.all_to_all(rows, "chan", split_axis=0, concat_axis=1, tiled=True)
    filled = conjugate_fill(mine, good, fg_cov)
    back = lax.all_to_all(filled, "chan", split_axis=1, concat_axis=0, tiled=True)
    return back.reshape(m_dev, 2, degrees, f_dev)


def solution(mesh):
    placed = (P("tm", "chan", None), P("tm", "chan", None, None, None), P(), P(), P())
    return jax.shard_map(
        per_device,
        mesh=mesh,
        in_specs=placed,
        out_specs=P("tm", None, None, "chan"),
        check_vma=False,
    )
```

```python
import functools
import math

import jax
import jax.numpy as jnp
from jax import lax
from jax.experimental import pallas as pl
from jax.experimental.pallas import tpu as pltpu
from jax.sharding import PartitionSpec as P

ITERS = 10
EPS = 1e-06
MESH = pl.DeviceIdType.MESH


def swap_groups(tiles):
    sub = lax.broadcasted_iota(jnp.int32, (8, 128), 0)
    lane = lax.broadcasted_iota(jnp.int32, (8, 128), 1)
    s1, l1 = (sub >= 4), (lane >= 64)
    s0, l0 = (sub % 4 >= 2), (lane % 64 >= 32)
    done = []
    for x in tiles:
        moved = pltpu.roll(pltpu.roll(x, 4, 0), 64, 1)
        x = jnp.where(s1 == l1, x, moved)
        up = pltpu.roll(pltpu.roll(x, 6, 0), 32, 1)
        down = pltpu.roll(pltpu.roll(x, 2, 0), 96, 1)
        x = jnp.where(s0 == l0, x, jnp.where(l0, up, down))
        done.append(x)
    return done


def kernel(
    n_tm, n_chan, m_ref, flags_ref, vis_hbm, beam_hbm, cov_hbm, out_ref,
    vis_v, beam_v, cov_v, pair_v, kron_v, part_v, got_v, give1, take1, give2, take2,
    local_sem, psend, precv, send1, recv1, send2, recv2,
):
    t_dev, f_dev, width = vis_v.shape
    half_w = width // 2
    n_m = m_ref.shape[0]
    m_dev = n_m // n_tm
    n_time = t_dev * n_tm
    fh = f_dev // 2
    n_f = cov_v.shape[0]
    my_tm = lax.axis_index("tm")
    my_chan = lax.axis_index("chan")

    barrier = pltpu.get_barrier_semaphore()
    for i in range(1, n_tm):
        pl.semaphore_signal(barrier, inc=1, device_id={"tm": lax.rem(my_tm + i, n_tm)}, device_id_type=MESH)

    @pl.loop(1, n_chan)
    def _(i):
        pl.semaphore_signal(barrier, inc=1, device_id={"chan": lax.rem(my_chan + i, n_chan)}, device_id_type=MESH)

    vis_copies = [
        pltpu.make_async_copy(
            vis_hbm.at[:, pl.ds(h * fh, fh), :], vis_v.at[:, pl.ds(h * fh, fh), :], local_sem.at[h]
        )
        for h in range(2)
    ]
    for copy in vis_copies:
        copy.start()

    row = lax.broadcasted_iota(jnp.int32, (n_m, t_dev), 0)
    modes = jnp.zeros((n_m, t_dev), jnp.int32)
    for k in range(n_m):
        modes = jnp.where(row == k, m_ref[k], modes)
    times = my_tm * t_dev + lax.broadcasted_iota(jnp.int32, (n_m, t_dev), 1)
    index = lax.rem(modes * times, n_time)
    angle = 2.0 * math.pi / n_time * index.astype(jnp.float32)
    wide = t_dev * fh
    spread = (
        lax.broadcasted_iota(jnp.int32, (t_dev, wide), 1) // fh == lax.broadcasted_iota(jnp.int32, (t_dev, wide), 0)
    ).astype(jnp.float32).astype(jnp.bfloat16)
    same = lax.broadcasted_iota(jnp.int32, (fh, wide), 1) % fh == lax.broadcasted_iota(jnp.int32, (fh, wide), 0)
    for q, table in enumerate((jnp.cos(angle), jnp.sin(angle))):
        lanes = jnp.dot(table.astype(jnp.bfloat16), spread, preferred_element_type=jnp.float32)
        for k in range(n_m):
            kron_v[q, k * fh : (k + 1) * fh, :] = jnp.where(same, lanes[k : k + 1, :], 0.0).astype(jnp.bfloat16)

    scale = 1.0 / math.sqrt(n_time)
    part_copies = []
    for h in range(2):
        vis_copies[h].wait()
        if h == 1:
            beam_copy = pltpu.make_async_copy(beam_hbm, beam_v, local_sem.at[2])
            cov_copy = pltpu.make_async_copy(cov_hbm, cov_v, local_sem.at[3])
            cov_copy.start()
            beam_copy.start()
        data = vis_v[:, h * fh : (h + 1) * fh, :].reshape(t_dev * fh, width)
        c = jnp.dot(kron_v[0], data, preferred_element_type=jnp.float32)
        s = jnp.dot(kron_v[1], data, preferred_element_type=jnp.float32)
        real = (c[:, :half_w] + s[:, half_w:]) * scale
        imag = (c[:, half_w:] - s[:, :half_w]) * scale
        part_v[:, h, :, :half_w] = real.reshape(n_tm, m_dev * fh, half_w)
        part_v[:, h, :, half_w:] = imag.reshape(n_tm, m_dev * fh, half_w)
        if h == 0:
            pl.semaphore_wait(barrier, n_tm - 1 + n_chan - 1)
        for i in range(1, n_tm):
            owner = lax.rem(my_tm + i, n_tm)
            copy = pltpu.make_async_remote_copy(
                src_ref=part_v.at[owner, h], dst_ref=got_v.at[i - 1, h],
                send_sem=psend.at[i - 1, h], recv_sem=precv.at[i - 1, h],
                device_id={"tm": owner}, device_id_type=MESH,
            )
            copy.start()
            part_copies.append(copy)

    cov_copy.wait()
    step = 64

    @pl.loop(0, n_f // step)
    def _(j):
        rows = pl.ds(pl.multiple_of(j * step, step), step)
        low_rows = pl.ds(pl.multiple_of(n_f + j * step, step), step)
        block = cov_v[rows, :]
        high = block.astype(jnp.bfloat16)
        pair_v[rows, :] = high
        pair_v[low_rows, :] = (block - high.astype(jnp.float32)).astype(jnp.bfloat16)

    beam_copy.wait()
    for copy in part_copies:
        copy.wait_recv()
    pieces = {}
    for h in range(2):
        total = part_v[my_tm, h]
        for i in range(n_tm - 1):
            total = total + got_v[i, h]
        mvis = total.astype(jnp.bfloat16).astype(jnp.float32)
        for m in range(m_dev):
            block = mvis[m * fh : (m + 1) * fh, :]
            pieces[(m, 0, h)] = block[:, :half_w]
            pieces[(m, 1, h)] = block[:, half_w:]
    against_real, against_imag = [], []
    for m in range(m_dev):
        for p in range(2):
            for h in range(2):
                against_real.append(pieces[(m, p, h)])
                against_imag.append(-pieces[(m, 1, h)] if p == 0 else pieces[(m, 0, h)])
    weights = jnp.concatenate(
        [jnp.concatenate(against_real, axis=0).T, jnp.concatenate(against_imag, axis=0).T], axis=0
    ).astype(jnp.bfloat16)

    degrees = beam_v.shape[3]
    lanes = 2 * m_dev * f_dev
    lane = lax.broadcasted_iota(jnp.int32, (degrees, lanes), 1)
    lane_id = lane // (2 * f_dev) * f_dev + lane % f_dev
    take = 4
    per_m = f_dev // take

    def project(j, acc):
        m = j // per_m
        f0 = (j - m * per_m) * take
        lhs = jnp.concatenate(
            [
                beam_v[m, pl.ds(f0, take), 0].reshape(take * degrees, half_w),
                beam_v[m, pl.ds(f0, take), 1].reshape(take * degrees, half_w),
            ],
            axis=1,
        )
        prod = jnp.dot(lhs, weights, preferred_element_type=jnp.float32)
        for i in range(take):
            acc = jnp.where(lane_id == m * f_dev + f0 + i, prod[i * degrees : (i + 1) * degrees, :], acc)
        return acc

    coeffs = lax.fori_loop(0, m_dev * per_m, project, jnp.zeros((degrees, lanes), jnp.float32))
    pair = degrees // n_chan
    give1[...] = coeffs.reshape(n_chan, pair, lanes)

    def exchange(give, got, ssem, rsem):
        def remote(i):
            peer = lax.rem(my_chan + i, n_chan)
            return pltpu.make_async_remote_copy(
                src_ref=give.at[peer], dst_ref=got.at[my_chan], send_sem=ssem.at[i], recv_sem=rsem.at[i],
                device_id={"chan": peer}, device_id_type=MESH,
            )

        @pl.loop(1, n_chan)
        def _(i):
            remote(i).start()

        own = pltpu.make_async_copy(give.at[my_chan], got.at[my_chan], ssem.at[0])
        own.start()
        own.wait()

        @pl.loop(1, n_chan)
        def _(i):
            remote(i).wait_recv()

    exchange(give1, take1, send1, recv1)
    mixed = take1[...].reshape(degrees, lanes)
    n_tiles = degrees // 8
    data = jnp.concatenate(swap_groups([mixed[8 * j : 8 * j + 8, :] for j in range(n_tiles)]), axis=1)
    good = jnp.broadcast_to((1 - flags_ref[...]).astype(jnp.float32), (8, n_f))

    def apply_cov(vec):
        high = vec.astype(jnp.bfloat16).astype(jnp.float32)
        both = jnp.concatenate([high, vec - high], axis=0).astype(jnp.bfloat16)
        prod = jnp.dot(jnp.concatenate([both, both], axis=1), pair_v[...], preferred_element_type=jnp.float32)
        return prod[:8, :] + prod[8:, :]

    def total_of(values):
        return jnp.sum(values, axis=1, keepdims=True)

    start = good * data

    def advance(step, carry):
        sol, resid, direc, norm_now = carry
        image = direc + good * apply_cov(direc)
        alpha = norm_now / (total_of(direc * image) + EPS)
        sol = sol + alpha * direc
        resid = resid - alpha * image
        norm_next = total_of(resid * resid)
        direc = resid + norm_next / (norm_now + EPS) * direc
        return (sol, resid, direc, norm_next)

    sol, _, _, _ = lax.fori_loop(0, ITERS, advance, (jnp.zeros_like(start), start, start, total_of(start * start)))
    filled = start + (1.0 - good) * apply_cov(sol)
    tiles = swap_groups([filled[:, 128 * j : 128 * (j + 1)] for j in range(n_tiles)])
    give2[...] = jnp.concatenate(tiles, axis=0).reshape(n_chan, pair, lanes)
    exchange(give2, take2, send2, recv2)
    back = take2[...].reshape(degrees, lanes)
    for m in range(m_dev):
        for p in range(2):
            at = (2 * m + p) * f_dev
            out_ref[m, p] = back[:, at : at + f_dev]

    for copy in part_copies:
        copy.wait_send()
    for give, got, ssem, rsem in ((give1, take1, send1, recv1), (give2, take2, send2, recv2)):

        @pl.loop(1, n_chan)
        def _(i):
            peer = lax.rem(my_chan + i, n_chan)
            pltpu.make_async_remote_copy(
                src_ref=give.at[peer], dst_ref=got.at[my_chan], send_sem=ssem.at[i], recv_sem=rsem.at[i],
                device_id={"chan": peer}, device_id_type=MESH,
            ).wait_send()


def per_device(n_tm, n_chan, vis, beam, fg_cov, flags, m_modes):
    t_dev, f_dev, width = vis.shape
    m_dev, _, _, degrees, half_w = beam.shape
    n_f = fg_cov.shape[0]
    lanes = 2 * m_dev * f_dev
    block = (n_chan, degrees // n_chan, lanes)
    any_space = pl.BlockSpec(memory_space=pl.ANY)
    return pl.pallas_call(
        functools.partial(kernel, n_tm, n_chan),
        out_shape=jax.ShapeDtypeStruct((m_dev, 2, degrees, f_dev), jnp.float32),
        in_specs=[
            pl.BlockSpec(memory_space=pltpu.SMEM),
            pl.BlockSpec(memory_space=pltpu.VMEM),
            any_space,
            any_space,
            any_space,
        ],
        out_specs=pl.BlockSpec(memory_space=pltpu.VMEM),
        scratch_shapes=[
            pltpu.VMEM(vis.shape, vis.dtype),
            pltpu.VMEM(beam.shape, beam.dtype),
            pltpu.VMEM(fg_cov.shape, jnp.float32),
            pltpu.VMEM((2 * n_f, n_f), jnp.bfloat16),
            pltpu.VMEM((2, m_dev * n_tm * f_dev // 2, t_dev * f_dev // 2), jnp.bfloat16),
            pltpu.VMEM((n_tm, 2, m_dev * f_dev // 2, width), jnp.float32),
            pltpu.VMEM((n_tm - 1, 2, m_dev * f_dev // 2, width), jnp.float32),
            pltpu.VMEM(block, jnp.float32),
            pltpu.VMEM(block, jnp.float32),
            pltpu.VMEM(block, jnp.float32),
            pltpu.VMEM(block, jnp.float32),
            pltpu.SemaphoreType.DMA((4,)),
            pltpu.SemaphoreType.DMA((n_tm - 1, 2)),
            pltpu.SemaphoreType.DMA((n_tm - 1, 2)),
            pltpu.SemaphoreType.DMA((n_chan,)),
            pltpu.SemaphoreType.DMA((n_chan,)),
            pltpu.SemaphoreType.DMA((n_chan,)),
            pltpu.SemaphoreType.DMA((n_chan,)),
        ],
        compiler_params=pltpu.CompilerParams(
            collective_id=0, has_side_effects=True, vmem_limit_bytes=48 * 1024 * 1024
        ),
    )(m_modes, flags.reshape(1, n_f), vis, beam, fg_cov)


def solution(mesh):
    placed = (P("tm", "chan", None), P("tm", "chan", None, None, None), P(), P(), P())
    return jax.shard_map(
        functools.partial(per_device, mesh.shape["tm"], mesh.shape["chan"]),
        mesh=mesh,
        in_specs=placed,
        out_specs=P("tm", None, None, "chan"),
        check_vma=False,
    )
```

```python
import functools
import math

import jax
import jax.numpy as jnp
from jax import lax
from jax.experimental import pallas as pl
from jax.experimental.pallas import tpu as pltpu
from jax.sharding import PartitionSpec as P

ITERS = 10
EPS = 1e-06
MESH = pl.DeviceIdType.MESH


def swap_groups(tiles):
    sub = lax.broadcasted_iota(jnp.int32, (8, 128), 0)
    lane = lax.broadcasted_iota(jnp.int32, (8, 128), 1)
    s1, l1 = (sub >= 4), (lane >= 64)
    s0, l0 = (sub % 4 >= 2), (lane % 64 >= 32)
    done = []
    for x in tiles:
        moved = pltpu.roll(pltpu.roll(x, 4, 0), 64, 1)
        x = jnp.where(s1 == l1, x, moved)
        up = pltpu.roll(pltpu.roll(x, 6, 0), 32, 1)
        down = pltpu.roll(pltpu.roll(x, 2, 0), 96, 1)
        x = jnp.where(s0 == l0, x, jnp.where(l0, up, down))
        done.append(x)
    return done


def kernel(
    n_tm, n_chan, m_hbm, flags_hbm, vis_hbm, beam_hbm, cov_hbm, out_ref,
    m_ref, flags_ref, vis_v, beam_v, cov_v, pair_v, kron_v, part_v, got_v, give1, take1, give2, take2,
    local_sem, psend, precv, send1, recv1, send2, recv2,
):
    t_dev, f_dev, width = vis_v.shape
    half_w = width // 2
    n_m = m_ref.shape[0]
    m_dev = n_m // n_tm
    n_time = t_dev * n_tm
    fh = f_dev // 2
    n_f = cov_v.shape[0]
    my_tm = lax.axis_index("tm")
    my_chan = lax.axis_index("chan")

    modes_copy = pltpu.make_async_copy(m_hbm, m_ref, local_sem.at[4])
    modes_copy.start()
    vis_copies = [
        pltpu.make_async_copy(
            vis_hbm.at[:, pl.ds(h * fh, fh), :], vis_v.at[:, pl.ds(h * fh, fh), :], local_sem.at[h]
        )
        for h in range(2)
    ]
    for copy in vis_copies:
        copy.start()
    flags_copy = pltpu.make_async_copy(flags_hbm, flags_ref, local_sem.at[5])
    flags_copy.start()

    barrier = pltpu.get_barrier_semaphore()
    for i in range(1, n_tm):
        pl.semaphore_signal(barrier, inc=1, device_id={"tm": lax.rem(my_tm + i, n_tm)}, device_id_type=MESH)
    for i in range(1, n_chan):
        pl.semaphore_signal(barrier, inc=1, device_id={"chan": lax.rem(my_chan + i, n_chan)}, device_id_type=MESH)

    modes_copy.wait()
    row = lax.broadcasted_iota(jnp.int32, (n_m, t_dev), 0)
    modes = jnp.zeros((n_m, t_dev), jnp.int32)
    for k in range(n_m):
        modes = jnp.where(row == k, m_ref[k], modes)
    times = my_tm * t_dev + lax.broadcasted_iota(jnp.int32, (n_m, t_dev), 1)
    index = lax.rem(modes * times, n_time)
    angle = 2.0 * math.pi / n_time * index.astype(jnp.float32)
    wide = t_dev * fh
    spread = (
        lax.broadcasted_iota(jnp.int32, (t_dev, wide), 1) // fh == lax.broadcasted_iota(jnp.int32, (t_dev, wide), 0)
    ).astype(jnp.float32).astype(jnp.bfloat16)
    same = lax.broadcasted_iota(jnp.int32, (fh, wide), 1) % fh == lax.broadcasted_iota(jnp.int32, (fh, wide), 0)
    for q, table in enumerate((jnp.cos(angle), jnp.sin(angle))):
        lanes = jnp.dot(table.astype(jnp.bfloat16), spread, preferred_element_type=jnp.float32)
        for k in range(n_m):
            kron_v[q, k * fh : (k + 1) * fh, :] = jnp.where(same, lanes[k : k + 1, :], 0.0).astype(jnp.bfloat16)

    scale = 1.0 / math.sqrt(n_time)
    part_copies = ([], [])
    for h in range(2):
        vis_copies[h].wait()
        if h == 1:
            beam_copy = pltpu.make_async_copy(beam_hbm, beam_v, local_sem.at[2])
            cov_copy = pltpu.make_async_copy(cov_hbm, cov_v, local_sem.at[3])
            cov_copy.start()
            beam_copy.start()
        data = vis_v[:, h * fh : (h + 1) * fh, :].reshape(t_dev * fh, width)
        c = jnp.dot(kron_v[0], data, preferred_element_type=jnp.float32)
        s = jnp.dot(kron_v[1], data, preferred_element_type=jnp.float32)
        real = (c[:, :half_w] + s[:, half_w:]) * scale
        imag = (c[:, half_w:] - s[:, :half_w]) * scale
        part_v[:, h, :, :half_w] = real.reshape(n_tm, m_dev * fh, half_w)
        part_v[:, h, :, half_w:] = imag.reshape(n_tm, m_dev * fh, half_w)
        if h == 0:
            pl.semaphore_wait(barrier, n_tm - 1 + n_chan - 1)
        for i in range(1, n_tm):
            owner = lax.rem(my_tm + i, n_tm)
            copy = pltpu.make_async_remote_copy(
                src_ref=part_v.at[owner, h], dst_ref=got_v.at[i - 1, h],
                send_sem=psend.at[i - 1, h], recv_sem=precv.at[i - 1, h],
                device_id={"tm": owner}, device_id_type=MESH,
            )
            copy.start()
            part_copies[h].append(copy)

    cov_copy.wait()
    step = 64

    @pl.loop(0, n_f // step)
    def _(j):
        rows = pl.ds(pl.multiple_of(j * step, step), step)
        low_rows = pl.ds(pl.multiple_of(n_f + j * step, step), step)
        block = cov_v[rows, :]
        high = block.astype(jnp.bfloat16)
        pair_v[rows, :] = high
        pair_v[low_rows, :] = (block - high.astype(jnp.float32)).astype(jnp.bfloat16)

    beam_copy.wait()
    degrees = beam_v.shape[3]
    lanes = 2 * m_dev * f_dev
    lane = lax.broadcasted_iota(jnp.int32, (degrees, lanes), 1)
    lane_id = lane // (2 * f_dev) * f_dev + lane % f_dev
    coeffs = jnp.zeros((degrees, lanes), jnp.float32)
    blank = jnp.zeros((fh, half_w), jnp.float32)
    for h in range(2):
        for copy in part_copies[h]:
            copy.wait_recv()
        total = part_v[my_tm, h]
        for i in range(n_tm - 1):
            total = total + got_v[i, h]
        mvis = total.astype(jnp.bfloat16).astype(jnp.float32)
        against_real, against_imag = [], []
        for m in range(m_dev):
            block = mvis[m * fh : (m + 1) * fh, :]
            re, im = block[:, :half_w], block[:, half_w:]
            for first, second in ((re, -im), (im, re)):
                against_real += [first, blank] if h == 0 else [blank, first]
                against_imag += [second, blank] if h == 0 else [blank, second]
        weights = jnp.concatenate(
            [jnp.concatenate(against_real, axis=0).T, jnp.concatenate(against_imag, axis=0).T], axis=0
        ).astype(jnp.bfloat16)
        for m in range(m_dev):
            rows = slice(h * fh, (h + 1) * fh)
            lhs = jnp.concatenate(
                [
                    beam_v[m, rows, 0].reshape(fh * degrees, half_w),
                    beam_v[m, rows, 1].reshape(fh * degrees, half_w),
                ],
                axis=1,
            )
            prod = jnp.dot(lhs, weights, preferred_element_type=jnp.float32)
            for i in range(fh):
                coeffs = jnp.where(
                    lane_id == m * f_dev + h * fh + i, prod[i * degrees : (i + 1) * degrees, :], coeffs
                )
    pair = degrees // n_chan
    give1[...] = coeffs.reshape(n_chan, pair, lanes)

    order = [n_chan // 2]
    for i in range(1, n_chan // 2):
        order += [n_chan // 2 - i, n_chan // 2 + i]

    def exchange(give, got, ssem, rsem):
        got[my_chan] = give[my_chan]
        for i in order:
            peer = lax.rem(my_chan + i, n_chan)
            pltpu.make_async_remote_copy(
                src_ref=give.at[peer], dst_ref=got.at[my_chan], send_sem=ssem.at[0], recv_sem=rsem.at[0],
                device_id={"chan": peer}, device_id_type=MESH,
            ).start()

    def wait_all(buf, sem):
        others = buf.at[pl.ds(0, n_chan - 1)]
        pltpu.make_async_copy(others, others, sem.at[0]).wait()

    exchange(give1, take1, send1, recv1)
    flags_copy.wait()
    wait_all(take1, recv1)
    mixed = take1[...].reshape(degrees, lanes)
    n_tiles = degrees // 8
    data = jnp.concatenate(swap_groups([mixed[8 * j : 8 * j + 8, :] for j in range(n_tiles)]), axis=1)
    good = jnp.broadcast_to((1 - flags_ref[...]).astype(jnp.float32), (8, n_f))

    def apply_cov(vec):
        high = vec.astype(jnp.bfloat16).astype(jnp.float32)
        both = jnp.concatenate([high, vec - high], axis=0).astype(jnp.bfloat16)
        prod = jnp.dot(jnp.concatenate([both, both], axis=1), pair_v[...], preferred_element_type=jnp.float32)
        return prod[:8, :] + prod[8:, :]

    def total_of(values):
        return jnp.sum(values, axis=1, keepdims=True)

    start = good * data

    def advance(step, carry):
        signal, resid, direc, norm_now = carry
        spread_out = apply_cov(direc)
        image = direc + good * spread_out
        alpha = norm_now / (total_of(direc * image) + EPS)
        signal = signal + alpha * spread_out
        resid = resid - alpha * image
        norm_next = total_of(resid * resid)
        direc = resid + norm_next / (norm_now + EPS) * direc
        return (signal, resid, direc, norm_next)

    signal, _, direc, norm_now = lax.fori_loop(
        0, ITERS - 1, advance, (jnp.zeros_like(start), start, start, total_of(start * start))
    )
    spread_out = apply_cov(direc)
    alpha = norm_now / (total_of(direc * (direc + good * spread_out)) + EPS)
    filled = start + (1.0 - good) * (signal + alpha * spread_out)
    tiles = swap_groups([filled[:, 128 * j : 128 * (j + 1)] for j in range(n_tiles)])
    give2[...] = jnp.concatenate(tiles, axis=0).reshape(n_chan, pair, lanes)
    exchange(give2, take2, send2, recv2)
    for copies in part_copies:
        for copy in copies:
            copy.wait_send()
    wait_all(give1, send1)
    wait_all(take2, recv2)
    back = take2[...].reshape(degrees, lanes)
    out_ref[...] = back.T.reshape(m_dev, 2, f_dev, degrees)
    wait_all(give2, send2)


def per_device(n_tm, n_chan, vis, beam, fg_cov, flags, m_modes):
    t_dev, f_dev, width = vis.shape
    m_dev, _, _, degrees, half_w = beam.shape
    n_f = fg_cov.shape[0]
    lanes = 2 * m_dev * f_dev
    block = (n_chan, degrees // n_chan, lanes)
    hbm = pl.BlockSpec(memory_space=pltpu.HBM)
    filled = pl.pallas_call(
        functools.partial(kernel, n_tm, n_chan),
        out_shape=jax.ShapeDtypeStruct((m_dev, 2, f_dev, degrees), jnp.float32),
        in_specs=[hbm] * 5,
        out_specs=pl.BlockSpec(memory_space=pltpu.VMEM),
        scratch_shapes=[
            pltpu.SMEM(m_modes.shape, jnp.int32),
            pltpu.VMEM((1, n_f), jnp.int32),
            pltpu.VMEM(vis.shape, vis.dtype),
            pltpu.VMEM(beam.shape, beam.dtype),
            pltpu.VMEM(fg_cov.shape, jnp.float32),
            pltpu.VMEM((2 * n_f, n_f), jnp.bfloat16),
            pltpu.VMEM((2, m_dev * n_tm * f_dev // 2, t_dev * f_dev // 2), jnp.bfloat16),
            pltpu.VMEM((n_tm, 2, m_dev * f_dev // 2, width), jnp.float32),
            pltpu.VMEM((n_tm - 1, 2, m_dev * f_dev // 2, width), jnp.float32),
            pltpu.VMEM(block, jnp.float32),
            pltpu.VMEM(block, jnp.float32),
            pltpu.VMEM(block, jnp.float32),
            pltpu.VMEM(block, jnp.float32),
            pltpu.SemaphoreType.DMA((6,)),
            pltpu.SemaphoreType.DMA((n_tm - 1, 2)),
            pltpu.SemaphoreType.DMA((n_tm - 1, 2)),
            pltpu.SemaphoreType.DMA((1,)),
            pltpu.SemaphoreType.DMA((1,)),
            pltpu.SemaphoreType.DMA((1,)),
            pltpu.SemaphoreType.DMA((1,)),
        ],
        compiler_params=pltpu.CompilerParams(
            collective_id=0, has_side_effects=True, vmem_limit_bytes=48 * 1024 * 1024
        ),
    )(*[pltpu.with_memory_space_constraint(a, pltpu.HBM) for a in (m_modes, flags.reshape(1, n_f), vis, beam, fg_cov)])
    return jnp.transpose(filled, (0, 1, 3, 2))


def solution(mesh):
    placed = (P("tm", "chan", None), P("tm", "chan", None, None, None), P(), P(), P())
    return jax.shard_map(
        functools.partial(per_device, mesh.shape["tm"], mesh.shape["chan"]),
        mesh=mesh,
        in_specs=placed,
        out_specs=P("tm", None, None, "chan"),
        check_vma=False,
    )
```

```python
import functools
import math

import jax
import jax.numpy as jnp
from jax import lax
from jax.experimental import pallas as pl
from jax.experimental.pallas import tpu as pltpu
from jax.sharding import PartitionSpec as P

ITERS = 10
EPS = 1e-06
MESH = pl.DeviceIdType.MESH


def swap_groups(tiles):
    sub = lax.broadcasted_iota(jnp.int32, (8, 128), 0)
    lane = lax.broadcasted_iota(jnp.int32, (8, 128), 1)
    s1, l1 = (sub >= 4), (lane >= 64)
    s0, l0 = (sub % 4 >= 2), (lane % 64 >= 32)
    done = []
    for x in tiles:
        moved = pltpu.roll(pltpu.roll(x, 4, 0), 64, 1)
        x = jnp.where(s1 == l1, x, moved)
        up = pltpu.roll(pltpu.roll(x, 6, 0), 32, 1)
        down = pltpu.roll(pltpu.roll(x, 2, 0), 96, 1)
        x = jnp.where(s0 == l0, x, jnp.where(l0, up, down))
        done.append(x)
    return done


def kernel(
    n_tm, n_chan, m_hbm, flags_hbm, vis_hbm, beam_hbm, cov_hbm, out_ref,
    m_ref, flags_ref, vis_v, beam_v, cov_v, pair_v, kron_v, part_v, got_y, sum_y, got_y2, got_x, sum_x, got_x2, give1, take1, give2, take2,
    local_sem, relay_sem, psend, precv, send1, recv1, send2, recv2,
):
    t_dev, f_dev, width = vis_v.shape
    half_w = width // 2
    n_m = m_ref.shape[0]
    m_dev = n_m // n_tm
    n_time = t_dev * n_tm
    fh = f_dev // 2
    n_f = cov_v.shape[0]
    my_tm = lax.axis_index("tm")
    my_chan = lax.axis_index("chan")

    modes_copy = pltpu.make_async_copy(m_hbm, m_ref, local_sem.at[4])
    modes_copy.start()
    vis_copies = [
        pltpu.make_async_copy(
            vis_hbm.at[:, pl.ds(h * fh, fh), :], vis_v.at[:, pl.ds(h * fh, fh), :], local_sem.at[h]
        )
        for h in range(2)
    ]
    for copy in vis_copies:
        copy.start()
    flags_copy = pltpu.make_async_copy(flags_hbm, flags_ref, local_sem.at[5])
    flags_copy.start()

    barrier = pltpu.get_barrier_semaphore()
    n_y = n_tm // 2
    my_x, my_y = my_tm // n_y, lax.rem(my_tm, n_y)
    n_w = 4
    n_z = n_chan // n_w
    my_z, my_w = my_chan // n_w, lax.rem(my_chan, n_w)

    def tm_at(dx, dy):
        return lax.rem(my_x + dx, 2) * n_y + lax.rem(my_y + dy, n_y)

    def chan_at(dz, dw):
        return lax.rem(my_z + dz, n_z) * n_w + lax.rem(my_w + dw, n_w)

    near_tm = [(1, 0)] + [(0, dy) for dy in range(1, n_y)]
    near_chan = [(dz, dw) for dz in (1, n_z - 1, 0) for dw in range(n_w) if (dz, dw) != (0, 0)]
    for dx, dy in near_tm:
        pl.semaphore_signal(barrier, inc=1, device_id={"tm": tm_at(dx, dy)}, device_id_type=MESH)
    for dz, dw in near_chan:
        pl.semaphore_signal(barrier, inc=1, device_id={"chan": chan_at(dz, dw)}, device_id_type=MESH)

    def relay(i, dz):
        for step in (dz, n_z - dz):
            pl.semaphore_signal(relay_sem.at[i], inc=1, device_id={"chan": chan_at(step, 0)}, device_id_type=MESH)

    modes_copy.wait()
    row = lax.broadcasted_iota(jnp.int32, (n_m, t_dev), 0)
    modes = jnp.zeros((n_m, t_dev), jnp.int32)
    for k in range(n_m):
        modes = jnp.where(row == k, m_ref[k], modes)
    times = my_tm * t_dev + lax.broadcasted_iota(jnp.int32, (n_m, t_dev), 1)
    index = lax.rem(modes * times, n_time)
    angle = 2.0 * math.pi / n_time * index.astype(jnp.float32)
    wide = t_dev * fh
    spread = (
        lax.broadcasted_iota(jnp.int32, (t_dev, wide), 1) // fh == lax.broadcasted_iota(jnp.int32, (t_dev, wide), 0)
    ).astype(jnp.float32).astype(jnp.bfloat16)
    same = lax.broadcasted_iota(jnp.int32, (fh, wide), 1) % fh == lax.broadcasted_iota(jnp.int32, (fh, wide), 0)
    for q, table in enumerate((jnp.cos(angle), jnp.sin(angle))):
        lanes = jnp.dot(table.astype(jnp.bfloat16), spread, preferred_element_type=jnp.float32)
        for k in range(n_m):
            kron_v[q, k * fh : (k + 1) * fh, :] = jnp.where(same, lanes[k : k + 1, :], 0.0).astype(jnp.bfloat16)

    scale = 1.0 / math.sqrt(n_time)
    far_first = [n_y // 2] + [dy for dy in range(1, n_y) if dy != n_y // 2]
    sent = []

    def push(src, dst, to):
        i = len(sent)
        copy = pltpu.make_async_remote_copy(
            src_ref=src, dst_ref=dst, send_sem=psend.at[i], recv_sem=precv.at[i],
            device_id={"tm": to}, device_id_type=MESH,
        )
        copy.start()
        sent.append(copy)
        return copy

    for h in range(2):
        vis_copies[h].wait()
        if h == 0:
            beam_copy = pltpu.make_async_copy(beam_hbm, beam_v, local_sem.at[2])
            cov_copy = pltpu.make_async_copy(cov_hbm, cov_v, local_sem.at[3])
            cov_copy.start()
            beam_copy.start()
        data = vis_v[:, h * fh : (h + 1) * fh, :].reshape(t_dev * fh, width)
        c = jnp.dot(kron_v[0], data, preferred_element_type=jnp.float32)
        s = jnp.dot(kron_v[1], data, preferred_element_type=jnp.float32)
        real = (c[:, :half_w] + s[:, half_w:]) * scale
        imag = (c[:, half_w:] - s[:, :half_w]) * scale
        part_v[:, h, :, :half_w] = real.reshape(n_tm, m_dev * fh, half_w)
        part_v[:, h, :, half_w:] = imag.reshape(n_tm, m_dev * fh, half_w)
        if h == 0:
            pl.semaphore_wait(barrier, len(near_tm) + len(near_chan))
            y_copies = [
                {dy: push(part_v.at[tm_at(rel, dy), 0], got_y.at[dy - 1, rel], tm_at(0, dy)) for dy in far_first}
                for rel in (1, 0)
            ]
            relay(0, 1)
        else:
            x_copies = {dy: push(part_v.at[tm_at(1, dy), 1], got_x.at[dy], tm_at(1, 0)) for dy in far_first}
    pl.semaphore_wait(relay_sem.at[0], 2)
    relay(1, 2)

    cov_copy.wait()
    step = 64

    @pl.loop(0, n_f // step)
    def _(j):
        rows = pl.ds(pl.multiple_of(j * step, step), step)
        low_rows = pl.ds(pl.multiple_of(n_f + j * step, step), step)
        block = cov_v[rows, :]
        high = block.astype(jnp.bfloat16)
        pair_v[rows, :] = high
        pair_v[low_rows, :] = (block - high.astype(jnp.float32)).astype(jnp.bfloat16)

    x2_copies, y2_copy = [], None
    for dy in far_first:
        x_copies[dy].wait_recv()
        sum_x[dy - 1] = part_v[tm_at(0, dy), 1] + got_x[dy]
        x2_copies.append(push(sum_x.at[dy - 1], got_x2.at[dy - 1], tm_at(0, dy)))
        if y2_copy is None:
            total = part_v[tm_at(1, 0), 0]
            for step in far_first:
                y_copies[0][step].wait_recv()
                total = total + got_y[step - 1, 1]
            sum_y[...] = total
            y2_copy = push(sum_y, got_y2, tm_at(1, 0))
            x_copies[0] = push(part_v.at[tm_at(1, 0), 1], got_x.at[0], tm_at(1, 0))
    beam_copy.wait()
    degrees = beam_v.shape[3]
    lanes = 2 * m_dev * f_dev
    lane = lax.broadcasted_iota(jnp.int32, (degrees, lanes), 1)
    lane_id = lane // (2 * f_dev) * f_dev + lane % f_dev
    coeffs = jnp.zeros((degrees, lanes), jnp.float32)
    blank = jnp.zeros((fh, half_w), jnp.float32)
    for h in range(2):
        total = part_v[my_tm, h]
        if h == 0:
            for dy in far_first:
                y_copies[1][dy].wait_recv()
                total = total + got_y[dy - 1, 0]
            y2_copy.wait_recv()
            total = total + got_y2[...]
        else:
            x_copies[0].wait_recv()
            total = total + got_x[0]
            for copy, dy in zip(x2_copies, far_first):
                copy.wait_recv()
                total = total + got_x2[dy - 1]
        mvis = total.astype(jnp.bfloat16).astype(jnp.float32)
        against_real, against_imag = [], []
        for m in range(m_dev):
            block = mvis[m * fh : (m + 1) * fh, :]
            re, im = block[:, :half_w], block[:, half_w:]
            for first, second in ((re, -im), (im, re)):
                against_real += [first, blank] if h == 0 else [blank, first]
                against_imag += [second, blank] if h == 0 else [blank, second]
        weights = jnp.concatenate(
            [jnp.concatenate(against_real, axis=0).T, jnp.concatenate(against_imag, axis=0).T], axis=0
        ).astype(jnp.bfloat16)
        for m in range(m_dev):
            rows = slice(h * fh, (h + 1) * fh)
            lhs = jnp.concatenate(
                [
                    beam_v[m, rows, 0].reshape(fh * degrees, half_w),
                    beam_v[m, rows, 1].reshape(fh * degrees, half_w),
                ],
                axis=1,
            )
            prod = jnp.dot(lhs, weights, preferred_element_type=jnp.float32)
            for i in range(fh):
                coeffs = jnp.where(
                    lane_id == m * f_dev + h * fh + i, prod[i * degrees : (i + 1) * degrees, :], coeffs
                )
    pl.semaphore_wait(relay_sem.at[1], 2)
    pair = degrees // n_chan
    give1[...] = coeffs.reshape(n_chan, pair, lanes)

    order = [n_chan // 2]
    for i in range(1, n_chan // 2):
        order += [n_chan // 2 - i, n_chan // 2 + i]

    def exchange(give, got, ssem, rsem):
        got[my_chan] = give[my_chan]
        for i in order:
            peer = lax.rem(my_chan + i, n_chan)
            pltpu.make_async_remote_copy(
                src_ref=give.at[peer], dst_ref=got.at[my_chan], send_sem=ssem.at[0], recv_sem=rsem.at[0],
                device_id={"chan": peer}, device_id_type=MESH,
            ).start()

    def wait_all(buf, sem):
        others = buf.at[pl.ds(0, n_chan - 1)]
        pltpu.make_async_copy(others, others, sem.at[0]).wait()

    exchange(give1, take1, send1, recv1)
    flags_copy.wait()
    wait_all(take1, recv1)
    mixed = take1[...].reshape(degrees, lanes)
    n_tiles = degrees // 8
    data = jnp.concatenate(swap_groups([mixed[8 * j : 8 * j + 8, :] for j in range(n_tiles)]), axis=1)
    good = jnp.broadcast_to((1 - flags_ref[...]).astype(jnp.float32), (8, n_f))

    def apply_cov(vec):
        high = vec.astype(jnp.bfloat16).astype(jnp.float32)
        both = jnp.concatenate([high, vec - high], axis=0).astype(jnp.bfloat16)
        prod = jnp.dot(jnp.concatenate([both, both], axis=1), pair_v[...], preferred_element_type=jnp.float32)
        return prod[:8, :] + prod[8:, :]

    def total_of(values):
        return jnp.sum(values, axis=1, keepdims=True)

    start = good * data

    def advance(step, carry):
        signal, resid, direc, norm_now = carry
        spread_out = apply_cov(direc)
        image = direc + good * spread_out
        alpha = norm_now / (total_of(direc * image) + EPS)
        signal = signal + alpha * spread_out
        resid = resid - alpha * image
        norm_next = total_of(resid * resid)
        direc = resid + norm_next / (norm_now + EPS) * direc
        return (signal, resid, direc, norm_next)

    signal, _, direc, norm_now = lax.fori_loop(
        0, ITERS - 1, advance, (jnp.zeros_like(start), start, start, total_of(start * start))
    )
    spread_out = apply_cov(direc)
    alpha = norm_now / (total_of(direc * (direc + good * spread_out)) + EPS)
    filled = start + (1.0 - good) * (signal + alpha * spread_out)
    tiles = swap_groups([filled[:, 128 * j : 128 * (j + 1)] for j in range(n_tiles)])
    give2[...] = jnp.concatenate(tiles, axis=0).reshape(n_chan, pair, lanes)
    exchange(give2, take2, send2, recv2)
    for copy in sent:
        copy.wait_send()
    wait_all(give1, send1)
    wait_all(take2, recv2)
    back = take2[...].reshape(degrees, lanes)
    out_ref[...] = back.T.reshape(m_dev, 2, f_dev, degrees)
    wait_all(give2, send2)


def per_device(n_tm, n_chan, vis, beam, fg_cov, flags, m_modes):
    t_dev, f_dev, width = vis.shape
    m_dev, _, _, degrees, half_w = beam.shape
    n_f = fg_cov.shape[0]
    lanes = 2 * m_dev * f_dev
    piece = (m_dev * f_dev // 2, width)
    block = (n_chan, degrees // n_chan, lanes)
    hbm = pl.BlockSpec(memory_space=pltpu.HBM)
    filled = pl.pallas_call(
        functools.partial(kernel, n_tm, n_chan),
        out_shape=jax.ShapeDtypeStruct((m_dev, 2, f_dev, degrees), jnp.float32),
        in_specs=[hbm] * 5,
        out_specs=pl.BlockSpec(memory_space=pltpu.VMEM),
        scratch_shapes=[
            pltpu.SMEM(m_modes.shape, jnp.int32),
            pltpu.VMEM((1, n_f), jnp.int32),
            pltpu.VMEM(vis.shape, vis.dtype),
            pltpu.VMEM(beam.shape, beam.dtype),
            pltpu.VMEM(fg_cov.shape, jnp.float32),
            pltpu.VMEM((2 * n_f, n_f), jnp.bfloat16),
            pltpu.VMEM((2, m_dev * n_tm * f_dev // 2, t_dev * f_dev // 2), jnp.bfloat16),
            pltpu.VMEM((n_tm, 2) + piece, jnp.float32),
            pltpu.VMEM((n_tm // 2 - 1, 2) + piece, jnp.float32),
            pltpu.VMEM(piece, jnp.float32),
            pltpu.VMEM(piece, jnp.float32),
            pltpu.VMEM((n_tm // 2,) + piece, jnp.float32),
            pltpu.VMEM((n_tm // 2 - 1,) + piece, jnp.float32),
            pltpu.VMEM((n_tm // 2 - 1,) + piece, jnp.float32),
            pltpu.VMEM(block, jnp.float32),
            pltpu.VMEM(block, jnp.float32),
            pltpu.VMEM(block, jnp.float32),
            pltpu.VMEM(block, jnp.float32),
            pltpu.SemaphoreType.DMA((6,)),
            pltpu.SemaphoreType.REGULAR((2,)),
            pltpu.SemaphoreType.DMA((14,)),
            pltpu.SemaphoreType.DMA((14,)),
            pltpu.SemaphoreType.DMA((1,)),
            pltpu.SemaphoreType.DMA((1,)),
            pltpu.SemaphoreType.DMA((1,)),
            pltpu.SemaphoreType.DMA((1,)),
        ],
        compiler_params=pltpu.CompilerParams(
            collective_id=0, has_side_effects=True, vmem_limit_bytes=48 * 1024 * 1024
        ),
    )(*[pltpu.with_memory_space_constraint(a, pltpu.HBM) for a in (m_modes, flags.reshape(1, n_f), vis, beam, fg_cov)])
    return jnp.transpose(filled, (0, 1, 3, 2))


def solution(mesh):
    placed = (P("tm", "chan", None), P("tm", "chan", None, None, None), P(), P(), P())
    return jax.shard_map(
        functools.partial(per_device, mesh.shape["tm"], mesh.shape["chan"]),
        mesh=mesh,
        in_specs=placed,
        out_specs=P("tm", None, None, "chan"),
        check_vma=False,
    )
```

```python
import functools
import math

import jax
import jax.numpy as jnp
from jax import lax
from jax.experimental import pallas as pl
from jax.experimental.pallas import tpu as pltpu
from jax.sharding import PartitionSpec as P

ITERS = 10
EPS = 1e-06
MESH = pl.DeviceIdType.MESH


def swap_groups(tiles):
    sub = lax.broadcasted_iota(jnp.int32, (8, 128), 0)
    lane = lax.broadcasted_iota(jnp.int32, (8, 128), 1)
    s1, l1 = (sub >= 4), (lane >= 64)
    s0, l0 = (sub % 4 >= 2), (lane % 64 >= 32)
    done = []
    for x in tiles:
        moved = pltpu.roll(pltpu.roll(x, 4, 0), 64, 1)
        x = jnp.where(s1 == l1, x, moved)
        up = pltpu.roll(pltpu.roll(x, 6, 0), 32, 1)
        down = pltpu.roll(pltpu.roll(x, 2, 0), 96, 1)
        x = jnp.where(s0 == l0, x, jnp.where(l0, up, down))
        done.append(x)
    return done


def kernel(
    n_tm, n_chan, m_hbm, flags_hbm, vis_hbm, beam_hbm, cov_hbm, out_ref,
    m_ref, flags_ref, vis_v, beam_v, cov_v, pair_v, kron_v, part_v, got_y, sum_y, last_y, got_x, sum_x, last_x, give1, take1, give2, take2,
    local_sem, vis_sem, relay_sem, psend, precv, send1, recv1, send2, recv2,
):
    t_dev, f_dev, width = vis_v.shape
    half_w = width // 2
    quarter = half_w // 2
    n_m = m_ref.shape[0]
    m_dev = n_m // n_tm
    n_time = t_dev * n_tm
    fh = f_dev // 2
    n_f = cov_v.shape[0]
    my_tm = lax.axis_index("tm")
    my_chan = lax.axis_index("chan")

    modes_copy = pltpu.make_async_copy(m_hbm, m_ref, local_sem.at[0])
    modes_copy.start()
    for h in range(2):
        rows = pl.ds(h * fh, fh)
        for j in range(2):
            for at in (j * quarter, half_w + j * quarter):
                pltpu.make_async_copy(
                    vis_hbm.at[:, rows, pl.ds(at, quarter)], vis_v.at[:, rows, pl.ds(at, quarter)],
                    vis_sem.at[2 * h + j],
                ).start()
    flags_copy = pltpu.make_async_copy(flags_hbm, flags_ref, local_sem.at[1])
    flags_copy.start()

    barrier = pltpu.get_barrier_semaphore()
    n_y = n_tm // 2
    my_x, my_y = my_tm // n_y, lax.rem(my_tm, n_y)
    n_w = 4
    n_z = n_chan // n_w
    my_z, my_w = my_chan // n_w, lax.rem(my_chan, n_w)

    def tm_at(dx, dy):
        return lax.rem(my_x + dx, 2) * n_y + lax.rem(my_y + dy, n_y)

    def chan_at(dz, dw):
        return lax.rem(my_z + dz, n_z) * n_w + lax.rem(my_w + dw, n_w)

    near_tm = [(1, 0)] + [(0, dy) for dy in range(1, n_y)]
    near_chan = [(dz, dw) for dz in (1, n_z - 1, 0) for dw in range(n_w) if (dz, dw) != (0, 0)]
    for dx, dy in near_tm:
        pl.semaphore_signal(barrier, inc=1, device_id={"tm": tm_at(dx, dy)}, device_id_type=MESH)
    for dz, dw in near_chan:
        pl.semaphore_signal(barrier, inc=1, device_id={"chan": chan_at(dz, dw)}, device_id_type=MESH)

    def relay(i, dz):
        for step in (dz, n_z - dz):
            pl.semaphore_signal(relay_sem.at[i], inc=1, device_id={"chan": chan_at(step, 0)}, device_id_type=MESH)

    modes_copy.wait()
    row = lax.broadcasted_iota(jnp.int32, (n_m, t_dev), 0)
    modes = jnp.zeros((n_m, t_dev), jnp.int32)
    for k in range(n_m):
        modes = jnp.where(row == k, m_ref[k], modes)
    times = my_tm * t_dev + lax.broadcasted_iota(jnp.int32, (n_m, t_dev), 1)
    index = lax.rem(modes * times, n_time)
    angle = 2.0 * math.pi / n_time * index.astype(jnp.float32)
    wide = t_dev * fh
    spread = (
        lax.broadcasted_iota(jnp.int32, (t_dev, wide), 1) // fh == lax.broadcasted_iota(jnp.int32, (t_dev, wide), 0)
    ).astype(jnp.float32).astype(jnp.bfloat16)
    same = lax.broadcasted_iota(jnp.int32, (fh, wide), 1) % fh == lax.broadcasted_iota(jnp.int32, (fh, wide), 0)
    for q, table in enumerate((jnp.cos(angle), jnp.sin(angle))):
        lanes = jnp.dot(table.astype(jnp.bfloat16), spread, preferred_element_type=jnp.float32)
        for k in range(n_m):
            kron_v[(q * n_m + k) * fh : (q * n_m + k + 1) * fh, :] = jnp.where(same, lanes[k : k + 1, :], 0.0).astype(jnp.bfloat16)

    scale = 1.0 / math.sqrt(n_time)
    far_first = [n_y // 2] + [dy for dy in range(1, n_y) if dy != n_y // 2]

    def push(src, dst, arrival, to):
        pltpu.make_async_remote_copy(
            src_ref=src, dst_ref=dst, send_sem=psend.at[0], recv_sem=precv.at[arrival],
            device_id={"tm": to}, device_id_type=MESH,
        ).start()

    def arrived(dst, arrival):
        pltpu.make_async_copy(dst, dst, precv.at[arrival]).wait()

    def push_y(h, rel, dy):
        to = (last_y.at[h, dy], 8 + h) if rel == 0 else (got_y.at[h, dy - 1], 6 + h)
        push(part_v.at[tm_at(rel, dy), 2 * h], *to, tm_at(0, dy))

    def push_x(h, dy):
        to = (last_x.at[h, 0], 10 + h) if dy == 0 else (got_x.at[h, dy - 1], 3 * h + dy - 1)
        push(part_v.at[tm_at(1, dy), 2 * h + 1], *to, tm_at(1, 0))

    for chunk in range(4):
        h, j = chunk // 2, chunk % 2
        both = vis_v.at[:, pl.ds(h * fh, fh), pl.ds(0, half_w)]
        pltpu.make_async_copy(both, both, vis_sem.at[chunk]).wait()
        if chunk == 0:
            beam_copy = pltpu.make_async_copy(beam_hbm, beam_v, local_sem.at[2])
            cov_copy = pltpu.make_async_copy(cov_hbm, cov_v, local_sem.at[3])
            cov_copy.start()
            beam_copy.start()
        data = jnp.concatenate(
            [
                vis_v[:, h * fh : (h + 1) * fh, at : at + quarter].reshape(t_dev * fh, quarter)
                for at in (j * quarter, half_w + j * quarter)
            ],
            axis=1,
        )
        prod = jnp.dot(kron_v[...], data, preferred_element_type=jnp.float32)
        c, s = prod[: n_m * fh, :], prod[n_m * fh :, :]
        real = (c[:, :quarter] + s[:, quarter:]) * scale
        imag = (c[:, quarter:] - s[:, :quarter]) * scale
        part_v[:, chunk, :, :quarter] = real.reshape(n_tm, m_dev * fh, quarter)
        part_v[:, chunk, :, quarter:] = imag.reshape(n_tm, m_dev * fh, quarter)
        if chunk == 0:
            pl.semaphore_wait(barrier, len(near_tm) + len(near_chan))
        if j == 0:
            for dy in far_first:
                push_y(h, 1, dy)
        else:
            for dy in far_first:
                push_x(h, dy)
        if chunk == 2:
            for dy in far_first:
                push_y(0, 0, dy)
        if chunk == 0:
            relay(0, 1)
    pl.semaphore_wait(relay_sem.at[0], 2)
    relay(1, 2)

    cov_copy.wait()
    step = 64

    @pl.loop(0, n_f // step)
    def _(j):
        rows = pl.ds(pl.multiple_of(j * step, step), step)
        low_rows = pl.ds(pl.multiple_of(n_f + j * step, step), step)
        block = cov_v[rows, :]
        high = block.astype(jnp.bfloat16)
        pair_v[rows, :] = high
        pair_v[low_rows, :] = (block - high.astype(jnp.float32)).astype(jnp.bfloat16)

    def forward_x(h, dy):
        arrived(got_x.at[h, dy - 1], 3 * h + dy - 1)
        sum_x[h, dy - 1] = part_v[tm_at(0, dy), 2 * h + 1] + got_x[h, dy - 1]
        push(sum_x.at[h, dy - 1], last_x.at[h, dy], 10 + h, tm_at(0, dy))

    def forward_y(h):
        arrived(got_y.at[h], 6 + h)
        total = part_v[tm_at(1, 0), 2 * h]
        for dy in range(1, n_y):
            total = total + got_y[h, dy - 1]
        sum_y[h] = total
        push(sum_y.at[h], last_y.at[h, 0], 8 + h, tm_at(1, 0))

    forward_x(0, far_first[0])
    forward_y(0)
    for dy in far_first[1:]:
        forward_x(0, dy)
    forward_y(1)
    push_x(0, 0)
    for dy in far_first:
        push_y(1, 0, dy)
        forward_x(1, dy)
    push_x(1, 0)
    beam_copy.wait()
    degrees = beam_v.shape[3]
    lanes = 2 * m_dev * f_dev
    lane = lax.broadcasted_iota(jnp.int32, (degrees, lanes), 1)
    lane_id = lane // (2 * f_dev) * f_dev + lane % f_dev
    coeffs = jnp.zeros((degrees, lanes), jnp.float32)
    blank = jnp.zeros((fh, quarter), jnp.float32)
    for chunk in range(4):
        h, j = chunk // 2, chunk % 2
        total = part_v[my_tm, chunk]
        last, arrival = ((last_y, 8), (last_x, 10))[j]
        arrived(last.at[h], arrival + h)
        for dy in range(n_y):
            total = total + last[h, dy]
        mvis = total.astype(jnp.bfloat16).astype(jnp.float32)
        against_real, against_imag = [], []
        for m in range(m_dev):
            re, im = mvis[m * fh : (m + 1) * fh, :quarter], mvis[m * fh : (m + 1) * fh, quarter:]
            for first, second in ((re, -im), (im, re)):
                against_real += [first, blank] if h == 0 else [blank, first]
                against_imag += [second, blank] if h == 0 else [blank, second]
        weights = jnp.concatenate(
            [jnp.concatenate(against_real, axis=0).T, jnp.concatenate(against_imag, axis=0).T], axis=0
        ).astype(jnp.bfloat16)
        for m in range(m_dev):
            lhs = jnp.concatenate(
                [
                    beam_v[m, h * fh : (h + 1) * fh, p, :, j * quarter : (j + 1) * quarter].reshape(fh * degrees, quarter)
                    for p in range(2)
                ],
                axis=1,
            )
            prod = jnp.dot(lhs, weights, preferred_element_type=jnp.float32)
            for i in range(fh):
                here = prod[i * degrees : (i + 1) * degrees, :]
                coeffs = jnp.where(
                    lane_id == m * f_dev + h * fh + i, here if j == 0 else coeffs + here, coeffs
                )
    pl.semaphore_wait(relay_sem.at[1], 2)
    pair = degrees // n_chan
    give1[...] = coeffs.reshape(n_chan, pair, lanes)

    order = [n_chan // 2]
    for i in range(1, n_chan // 2):
        order += [n_chan // 2 - i, n_chan // 2 + i]

    def exchange(give, got, ssem, rsem):
        got[my_chan] = give[my_chan]
        for i in order:
            peer = lax.rem(my_chan + i, n_chan)
            pltpu.make_async_remote_copy(
                src_ref=give.at[peer], dst_ref=got.at[my_chan], send_sem=ssem.at[0], recv_sem=rsem.at[0],
                device_id={"chan": peer}, device_id_type=MESH,
            ).start()

    def wait_all(buf, sem):
        others = buf.at[pl.ds(0, n_chan - 1)]
        pltpu.make_async_copy(others, others, sem.at[0]).wait()

    exchange(give1, take1, send1, recv1)
    flags_copy.wait()
    wait_all(take1, recv1)
    mixed = take1[...].reshape(degrees, lanes)
    n_tiles = degrees // 8
    data = jnp.concatenate(swap_groups([mixed[8 * j : 8 * j + 8, :] for j in range(n_tiles)]), axis=1)
    good = jnp.broadcast_to((1 - flags_ref[...]).astype(jnp.float32), (8, n_f))

    def apply_cov(vec):
        high = vec.astype(jnp.bfloat16).astype(jnp.float32)
        both = jnp.concatenate([high, vec - high], axis=0).astype(jnp.bfloat16)
        prod = jnp.dot(jnp.concatenate([both, both], axis=1), pair_v[...], preferred_element_type=jnp.float32)
        return prod[:8, :] + prod[8:, :]

    def total_of(values):
        return jnp.sum(values, axis=1, keepdims=True)

    start = good * data

    def advance(step, carry):
        signal, resid, direc, norm_now = carry
        spread_out = apply_cov(direc)
        image = direc + good * spread_out
        alpha = norm_now / (total_of(direc * image) + EPS)
        signal = signal + alpha * spread_out
        resid = resid - alpha * image
        norm_next = total_of(resid * resid)
        direc = resid + norm_next / (norm_now + EPS) * direc
        return (signal, resid, direc, norm_next)

    signal, _, direc, norm_now = lax.fori_loop(
        0, ITERS - 1, advance, (jnp.zeros_like(start), start, start, total_of(start * start)), unroll=True
    )
    spread_out = apply_cov(direc)
    alpha = norm_now / (total_of(direc * (direc + good * spread_out)) + EPS)
    filled = start + (1.0 - good) * (signal + alpha * spread_out)
    tiles = swap_groups([filled[:, 128 * j : 128 * (j + 1)] for j in range(n_tiles)])
    give2[...] = jnp.concatenate(tiles, axis=0).reshape(n_chan, pair, lanes)
    exchange(give2, take2, send2, recv2)
    all_sent = part_v.at[pl.ds(0, n_tm - 1)]
    pltpu.make_async_copy(all_sent, all_sent, psend.at[0]).wait()
    wait_all(give1, send1)
    wait_all(take2, recv2)
    back = take2[...].reshape(degrees, lanes)
    out_ref[...] = back.T.reshape(m_dev, 2, f_dev, degrees)
    wait_all(give2, send2)


def per_device(n_tm, n_chan, vis, beam, fg_cov, flags, m_modes):
    t_dev, f_dev, width = vis.shape
    m_dev, _, _, degrees, half_w = beam.shape
    n_f = fg_cov.shape[0]
    lanes = 2 * m_dev * f_dev
    piece = (m_dev * f_dev // 2, width // 2)
    block = (n_chan, degrees // n_chan, lanes)
    hbm = pl.BlockSpec(memory_space=pltpu.HBM)
    filled = pl.pallas_call(
        functools.partial(kernel, n_tm, n_chan),
        out_shape=jax.ShapeDtypeStruct((m_dev, 2, f_dev, degrees), jnp.float32),
        in_specs=[hbm] * 5,
        out_specs=pl.BlockSpec(memory_space=pltpu.VMEM),
        scratch_shapes=[
            pltpu.SMEM(m_modes.shape, jnp.int32),
            pltpu.VMEM((1, n_f), jnp.int32),
            pltpu.VMEM(vis.shape, vis.dtype),
            pltpu.VMEM(beam.shape, beam.dtype),
            pltpu.VMEM(fg_cov.shape, jnp.float32),
            pltpu.VMEM((2 * n_f, n_f), jnp.bfloat16),
            pltpu.VMEM((m_dev * n_tm * f_dev, t_dev * f_dev // 2), jnp.bfloat16),
            pltpu.VMEM((n_tm, 4) + piece, jnp.float32),
            pltpu.VMEM((2, n_tm // 2 - 1) + piece, jnp.float32),
            pltpu.VMEM((2,) + piece, jnp.float32),
            pltpu.VMEM((2, n_tm // 2) + piece, jnp.float32),
            pltpu.VMEM((2, n_tm // 2 - 1) + piece, jnp.float32),
            pltpu.VMEM((2, n_tm // 2 - 1) + piece, jnp.float32),
            pltpu.VMEM((2, n_tm // 2) + piece, jnp.float32),
            pltpu.VMEM(block, jnp.float32),
            pltpu.VMEM(block, jnp.float32),
            pltpu.VMEM(block, jnp.float32),
            pltpu.VMEM(block, jnp.float32),
            pltpu.SemaphoreType.DMA((4,)),
            pltpu.SemaphoreType.DMA((4,)),
            pltpu.SemaphoreType.REGULAR((2,)),
            pltpu.SemaphoreType.DMA((1,)),
            pltpu.SemaphoreType.DMA((12,)),
            pltpu.SemaphoreType.DMA((1,)),
            pltpu.SemaphoreType.DMA((1,)),
            pltpu.SemaphoreType.DMA((1,)),
            pltpu.SemaphoreType.DMA((1,)),
        ],
        compiler_params=pltpu.CompilerParams(
            collective_id=0, has_side_effects=True, vmem_limit_bytes=48 * 1024 * 1024
        ),
    )(*[pltpu.with_memory_space_constraint(a, pltpu.HBM) for a in (m_modes, flags.reshape(1, n_f), vis, beam, fg_cov)])
    return jnp.transpose(filled, (0, 1, 3, 2))


def solution(mesh):
    placed = (P("tm", "chan", None), P("tm", "chan", None, None, None), P(), P(), P())
    return jax.shard_map(
        functools.partial(per_device, mesh.shape["tm"], mesh.shape["chan"]),
        mesh=mesh,
        in_specs=placed,
        out_specs=P("tm", None, None, "chan"),
        check_vma=False,
    )
```

```python
import functools
import math

import jax
import jax.numpy as jnp
from jax import lax
from jax.experimental import pallas as pl
from jax.experimental.pallas import tpu as pltpu
from jax.sharding import PartitionSpec as P

ITERS = 10
EPS = 1e-06
MESH = pl.DeviceIdType.MESH


def swap_groups(tiles):
    sub = lax.broadcasted_iota(jnp.int32, (8, 128), 0)
    lane = lax.broadcasted_iota(jnp.int32, (8, 128), 1)
    s1, l1 = (sub >= 4), (lane >= 64)
    s0, l0 = (sub % 4 >= 2), (lane % 64 >= 32)
    done = []
    for x in tiles:
        moved = pltpu.roll(pltpu.roll(x, 4, 0), 64, 1)
        x = jnp.where(s1 == l1, x, moved)
        up = pltpu.roll(pltpu.roll(x, 6, 0), 32, 1)
        down = pltpu.roll(pltpu.roll(x, 2, 0), 96, 1)
        x = jnp.where(s0 == l0, x, jnp.where(l0, up, down))
        done.append(x)
    return done


def kernel(
    n_tm, n_chan, m_hbm, flags_hbm, vis_hbm, beam_hbm, cov_hbm, out_ref,
    m_ref, flags_ref, vis_v, beam_v, cov_v, pair_v, kron_v, part_v, got_y, sum_y, last_y, got_x, sum_x, last_x, give1, take1, give2, take2,
    local_sem, vis_sem, relay_sem, psend, precv, send1, recv1, send2, recv2,
):
    t_dev, f_dev, width = vis_v.shape
    half_w = width // 2
    quarter = half_w // 2
    n_m = m_ref.shape[0]
    m_dev = n_m // n_tm
    n_time = t_dev * n_tm
    fh = f_dev // 2
    n_f = cov_v.shape[0]
    my_tm = lax.axis_index("tm")
    my_chan = lax.axis_index("chan")

    modes_copy = pltpu.make_async_copy(m_hbm, m_ref, local_sem.at[0])
    modes_copy.start()
    def fetch(chunk):
        h, j = chunk // 2, chunk % 2
        rows = pl.ds(h * fh, fh)
        for at in (j * quarter, half_w + j * quarter):
            pltpu.make_async_copy(
                vis_hbm.at[:, rows, pl.ds(at, quarter)], vis_v.at[:, rows, pl.ds(at, quarter)], vis_sem.at[chunk]
            ).start()

    fetch(0)
    barrier = pltpu.get_barrier_semaphore()
    n_y = n_tm // 2
    my_x, my_y = my_tm // n_y, lax.rem(my_tm, n_y)
    n_w = 4
    n_z = n_chan // n_w
    my_z, my_w = my_chan // n_w, lax.rem(my_chan, n_w)

    def tm_at(dx, dy):
        return lax.rem(my_x + dx, 2) * n_y + lax.rem(my_y + dy, n_y)

    def chan_at(dz, dw):
        return lax.rem(my_z + dz, n_z) * n_w + lax.rem(my_w + dw, n_w)

    near_tm = [(1, 0)] + [(0, dy) for dy in range(1, n_y)]
    near_chan = [(dz, dw) for dz in (1, n_z - 1, 0) for dw in range(n_w) if (dz, dw) != (0, 0)]
    for dx, dy in near_tm:
        pl.semaphore_signal(barrier, inc=1, device_id={"tm": tm_at(dx, dy)}, device_id_type=MESH)
    for dz, dw in near_chan:
        pl.semaphore_signal(barrier, inc=1, device_id={"chan": chan_at(dz, dw)}, device_id_type=MESH)

    def relay(i, dz):
        for step in (dz, n_z - dz):
            pl.semaphore_signal(relay_sem.at[i], inc=1, device_id={"chan": chan_at(step, 0)}, device_id_type=MESH)

    for chunk in range(1, 4):
        fetch(chunk)
    flags_copy = pltpu.make_async_copy(flags_hbm, flags_ref, local_sem.at[1])
    flags_copy.start()

    modes_copy.wait()
    row = lax.broadcasted_iota(jnp.int32, (n_m, t_dev), 0)
    modes = jnp.zeros((n_m, t_dev), jnp.int32)
    for k in range(n_m):
        modes = jnp.where(row == k, m_ref[k], modes)
    times = my_tm * t_dev + lax.broadcasted_iota(jnp.int32, (n_m, t_dev), 1)
    index = lax.rem(modes * times, n_time)
    angle = 2.0 * math.pi / n_time * index.astype(jnp.float32)
    wide = t_dev * fh
    spread = (
        lax.broadcasted_iota(jnp.int32, (t_dev, wide), 1) // fh == lax.broadcasted_iota(jnp.int32, (t_dev, wide), 0)
    ).astype(jnp.float32).astype(jnp.bfloat16)
    same = lax.broadcasted_iota(jnp.int32, (fh, wide), 1) % fh == lax.broadcasted_iota(jnp.int32, (fh, wide), 0)
    for q, table in enumerate((jnp.cos(angle), jnp.sin(angle))):
        lanes = jnp.dot(table.astype(jnp.bfloat16), spread, preferred_element_type=jnp.float32)
        for k in range(n_m):
            kron_v[(q * n_m + k) * fh : (q * n_m + k + 1) * fh, :] = jnp.where(same, lanes[k : k + 1, :], 0.0).astype(jnp.bfloat16)

    scale = 1.0 / math.sqrt(n_time)
    far_first = [n_y // 2] + [dy for dy in range(1, n_y) if dy != n_y // 2]

    def push(src, dst, arrival, to):
        pltpu.make_async_remote_copy(
            src_ref=src, dst_ref=dst, send_sem=psend.at[0], recv_sem=precv.at[arrival],
            device_id={"tm": to}, device_id_type=MESH,
        ).start()

    def arrived(dst, arrival):
        pltpu.make_async_copy(dst, dst, precv.at[arrival]).wait()

    def push_y(h, rel, dy):
        to = (last_y.at[h, dy], 8 + h) if rel == 0 else (got_y.at[h, dy - 1], 6 + h)
        push(part_v.at[tm_at(rel, dy), 2 * h], *to, tm_at(0, dy))

    def push_x(h, dy):
        to = (last_x.at[h, 0], 10 + h) if dy == 0 else (got_x.at[h, dy - 1], 3 * h + dy - 1)
        push(part_v.at[tm_at(1, dy), 2 * h + 1], *to, tm_at(1, 0))

    for chunk in range(4):
        h, j = chunk // 2, chunk % 2
        both = vis_v.at[:, pl.ds(h * fh, fh), pl.ds(0, half_w)]
        pltpu.make_async_copy(both, both, vis_sem.at[chunk]).wait()
        if chunk == 0:
            beam_copy = pltpu.make_async_copy(beam_hbm, beam_v, local_sem.at[2])
            cov_copy = pltpu.make_async_copy(cov_hbm, cov_v, local_sem.at[3])
            cov_copy.start()
            beam_copy.start()
        data = jnp.concatenate(
            [
                vis_v[:, h * fh : (h + 1) * fh, at : at + quarter].reshape(t_dev * fh, quarter)
                for at in (j * quarter, half_w + j * quarter)
            ],
            axis=1,
        )
        prod = jnp.dot(kron_v[...], data, preferred_element_type=jnp.float32)
        c, s = prod[: n_m * fh, :], prod[n_m * fh :, :]
        real = (c[:, :quarter] + s[:, quarter:]) * scale
        imag = (c[:, quarter:] - s[:, :quarter]) * scale
        part_v[:, chunk, :, :quarter] = real.reshape(n_tm, m_dev * fh, quarter)
        part_v[:, chunk, :, quarter:] = imag.reshape(n_tm, m_dev * fh, quarter)
        if chunk == 0:
            pl.semaphore_wait(barrier, len(near_tm) + len(near_chan))
        if j == 0:
            for dy in far_first:
                push_y(h, 1, dy)
        else:
            for dy in far_first:
                push_x(h, dy)
            if h == 1:
                push_x(0, 0)
        if chunk == 2:
            for dy in far_first:
                push_y(0, 0, dy)
        if chunk == 0:
            relay(0, 1)
    pl.semaphore_wait(relay_sem.at[0], 2)
    relay(1, 2)

    cov_copy.wait()
    step = 64

    @pl.loop(0, n_f // step)
    def _(j):
        rows = pl.ds(pl.multiple_of(j * step, step), step)
        low_rows = pl.ds(pl.multiple_of(n_f + j * step, step), step)
        block = cov_v[rows, :]
        high = block.astype(jnp.bfloat16)
        pair_v[rows, :] = high
        pair_v[low_rows, :] = (block - high.astype(jnp.float32)).astype(jnp.bfloat16)

    def forward_x(h, dy):
        arrived(got_x.at[h, dy - 1], 3 * h + dy - 1)
        sum_x[h, dy - 1] = part_v[tm_at(0, dy), 2 * h + 1] + got_x[h, dy - 1]
        push(sum_x.at[h, dy - 1], last_x.at[h, dy], 10 + h, tm_at(0, dy))

    def forward_y(h):
        arrived(got_y.at[h], 6 + h)
        total = part_v[tm_at(1, 0), 2 * h]
        for dy in range(1, n_y):
            total = total + got_y[h, dy - 1]
        sum_y[h] = total
        push(sum_y.at[h], last_y.at[h, 0], 8 + h, tm_at(1, 0))

    forward_x(0, far_first[0])
    forward_y(0)
    for dy in far_first[1:]:
        forward_x(0, dy)
    forward_y(1)
    for dy in far_first:
        push_y(1, 0, dy)
        forward_x(1, dy)
    push_x(1, 0)
    beam_copy.wait()
    degrees = beam_v.shape[3]
    lanes = 2 * m_dev * f_dev
    lane = lax.broadcasted_iota(jnp.int32, (degrees, lanes), 1)
    lane_id = lane // (2 * f_dev) * f_dev + lane % f_dev
    coeffs = jnp.zeros((degrees, lanes), jnp.float32)
    blank = jnp.zeros((fh, quarter), jnp.float32)
    for chunk in (1, 0, 2, 3):
        h, j = chunk // 2, chunk % 2
        first_of_half = chunk in (1, 2)
        total = part_v[my_tm, chunk]
        last, arrival = ((last_y, 8), (last_x, 10))[j]
        arrived(last.at[h], arrival + h)
        for dy in range(n_y):
            total = total + last[h, dy]
        mvis = total.astype(jnp.bfloat16).astype(jnp.float32)
        against_real, against_imag = [], []
        for m in range(m_dev):
            re, im = mvis[m * fh : (m + 1) * fh, :quarter], mvis[m * fh : (m + 1) * fh, quarter:]
            for first, second in ((re, -im), (im, re)):
                against_real += [first, blank] if h == 0 else [blank, first]
                against_imag += [second, blank] if h == 0 else [blank, second]
        weights = jnp.concatenate(
            [jnp.concatenate(against_real, axis=0).T, jnp.concatenate(against_imag, axis=0).T], axis=0
        ).astype(jnp.bfloat16)
        for m in range(m_dev):
            lhs = jnp.concatenate(
                [
                    beam_v[m, h * fh : (h + 1) * fh, p, :, j * quarter : (j + 1) * quarter].reshape(fh * degrees, quarter)
                    for p in range(2)
                ],
                axis=1,
            )
            prod = jnp.dot(lhs, weights, preferred_element_type=jnp.float32)
            for i in range(fh):
                here = prod[i * degrees : (i + 1) * degrees, :]
                coeffs = jnp.where(
                    lane_id == m * f_dev + h * fh + i, here if first_of_half else coeffs + here, coeffs
                )
    pl.semaphore_wait(relay_sem.at[1], 2)
    pair = degrees // n_chan
    give1[...] = coeffs.reshape(n_chan, pair, lanes)

    order = [n_chan // 2]
    for i in range(1, n_chan // 2):
        order += [n_chan // 2 - i, n_chan // 2 + i]

    def exchange(give, got, ssem, rsem):
        got[my_chan] = give[my_chan]
        for i in order:
            peer = lax.rem(my_chan + i, n_chan)
            pltpu.make_async_remote_copy(
                src_ref=give.at[peer], dst_ref=got.at[my_chan], send_sem=ssem.at[0], recv_sem=rsem.at[0],
                device_id={"chan": peer}, device_id_type=MESH,
            ).start()

    def wait_all(buf, sem):
        others = buf.at[pl.ds(0, n_chan - 1)]
        pltpu.make_async_copy(others, others, sem.at[0]).wait()

    exchange(give1, take1, send1, recv1)
    flags_copy.wait()
    wait_all(take1, recv1)
    mixed = take1[...].reshape(degrees, lanes)
    n_tiles = degrees // 8
    data = jnp.concatenate(swap_groups([mixed[8 * j : 8 * j + 8, :] for j in range(n_tiles)]), axis=1)
    good = jnp.broadcast_to((1 - flags_ref[...]).astype(jnp.float32), (8, n_f))

    def apply_cov(vec):
        high = vec.astype(jnp.bfloat16).astype(jnp.float32)
        both = jnp.concatenate([high, vec - high], axis=0).astype(jnp.bfloat16)
        prod = jnp.dot(jnp.concatenate([both, both], axis=1), pair_v[...], preferred_element_type=jnp.float32)
        return prod[:8, :] + prod[8:, :]

    def total_of(values):
        return jnp.sum(values, axis=1, keepdims=True)

    start = good * data

    def advance(step, carry):
        signal, resid, direc, norm_now = carry
        spread_out = apply_cov(direc)
        image = direc + good * spread_out
        alpha = norm_now / (total_of(direc * image) + EPS)
        signal = signal + alpha * spread_out
        resid = resid - alpha * image
        norm_next = total_of(resid * resid)
        direc = resid + norm_next / (norm_now + EPS) * direc
        return (signal, resid, direc, norm_next)

    signal, _, direc, norm_now = lax.fori_loop(
        0, ITERS - 1, advance, (jnp.zeros_like(start), start, start, total_of(start * start)), unroll=True
    )
    spread_out = apply_cov(direc)
    alpha = norm_now / (total_of(direc * (direc + good * spread_out)) + EPS)
    filled = start + (1.0 - good) * (signal + alpha * spread_out)
    tiles = swap_groups([filled[:, 128 * j : 128 * (j + 1)] for j in range(n_tiles)])
    give2[...] = jnp.concatenate(tiles, axis=0).reshape(n_chan, pair, lanes)
    exchange(give2, take2, send2, recv2)
    all_sent = part_v.at[pl.ds(0, n_tm - 1)]
    pltpu.make_async_copy(all_sent, all_sent, psend.at[0]).wait()
    wait_all(give1, send1)
    wait_all(take2, recv2)
    back = take2[...].reshape(degrees, lanes)
    out_ref[...] = back.T.reshape(m_dev, 2, f_dev, degrees)
    wait_all(give2, send2)


def per_device(n_tm, n_chan, vis, beam, fg_cov, flags, m_modes):
    t_dev, f_dev, width = vis.shape
    m_dev, _, _, degrees, half_w = beam.shape
    n_f = fg_cov.shape[0]
    lanes = 2 * m_dev * f_dev
    piece = (m_dev * f_dev // 2, width // 2)
    block = (n_chan, degrees // n_chan, lanes)
    hbm = pl.BlockSpec(memory_space=pltpu.HBM)
    filled = pl.pallas_call(
        functools.partial(kernel, n_tm, n_chan),
        out_shape=jax.ShapeDtypeStruct((m_dev, 2, f_dev, degrees), jnp.float32),
        in_specs=[hbm] * 5,
        out_specs=pl.BlockSpec(memory_space=pltpu.VMEM),
        scratch_shapes=[
            pltpu.SMEM(m_modes.shape, jnp.int32),
            pltpu.VMEM((1, n_f), jnp.int32),
            pltpu.VMEM(vis.shape, vis.dtype),
            pltpu.VMEM(beam.shape, beam.dtype),
            pltpu.VMEM(fg_cov.shape, jnp.float32),
            pltpu.VMEM((2 * n_f, n_f), jnp.bfloat16),
            pltpu.VMEM((m_dev * n_tm * f_dev, t_dev * f_dev // 2), jnp.bfloat16),
            pltpu.VMEM((n_tm, 4) + piece, jnp.float32),
            pltpu.VMEM((2, n_tm // 2 - 1) + piece, jnp.float32),
            pltpu.VMEM((2,) + piece, jnp.float32),
            pltpu.VMEM((2, n_tm // 2) + piece, jnp.float32),
            pltpu.VMEM((2, n_tm // 2 - 1) + piece, jnp.float32),
            pltpu.VMEM((2, n_tm // 2 - 1) + piece, jnp.float32),
            pltpu.VMEM((2, n_tm // 2) + piece, jnp.float32),
            pltpu.VMEM(block, jnp.float32),
            pltpu.VMEM(block, jnp.float32),
            pltpu.VMEM(block, jnp.float32),
            pltpu.VMEM(block, jnp.float32),
            pltpu.SemaphoreType.DMA((4,)),
            pltpu.SemaphoreType.DMA((4,)),
            pltpu.SemaphoreType.REGULAR((2,)),
            pltpu.SemaphoreType.DMA((1,)),
            pltpu.SemaphoreType.DMA((12,)),
            pltpu.SemaphoreType.DMA((1,)),
            pltpu.SemaphoreType.DMA((1,)),
            pltpu.SemaphoreType.DMA((1,)),
            pltpu.SemaphoreType.DMA((1,)),
        ],
        compiler_params=pltpu.CompilerParams(
            collective_id=0, has_side_effects=True, vmem_limit_bytes=48 * 1024 * 1024
        ),
    )(*[pltpu.with_memory_space_constraint(a, pltpu.HBM) for a in (m_modes, flags.reshape(1, n_f), vis, beam, fg_cov)])
    return jnp.transpose(filled, (0, 1, 3, 2))


def solution(mesh):
    placed = (P("tm", "chan", None), P("tm", "chan", None, None, None), P(), P(), P())
    return jax.shard_map(
        functools.partial(per_device, mesh.shape["tm"], mesh.shape["chan"]),
        mesh=mesh,
        in_specs=placed,
        out_specs=P("tm", None, None, "chan"),
        check_vma=False,
    )
```
